32 devices in a mesh: expert: 16 (over z, y, x), replica: 2 (over core).
Axes of the slice: x: 2, y: 2, z: 4, core: 2. Of those that a mesh axis runs over, the one named last changes fastest.
Arguments:
- grad_tokens: bfloat16 [4096, 3584], P(('expert', 'replica')), may hold values from -1.5 to 1.5
- gates: float32 [4096, 8], P(('expert', 'replica')), may hold values from 0.02 to 0.3
- expert_ids: int32 [4096, 8], P(('expert', 'replica')), may hold values from 0 to 15, all different within a row; in each aligned block of 128 rows (0 to 127, 128 to 255, ...) at most 80 rows name the same one
- hidden: bfloat16 [16, 2560, 1024], P('expert', 'replica'), may hold values from -11 to 11
- row_moment: float32 [16, 1024], P('expert', 'replica'), may hold values from 0.1 to 1
- col_moment: float32 [16, 3584], P('expert'), may hold values from 0.1 to 1
Outputs:
- update: bfloat16 [16, 1024, 3584], P('expert', 'replica')
- row_new: float32 [16, 1024], P('expert', 'replica')
- col_new: float32 [16, 3584], P('expert')
The draws below stay inside these ranges and needn't reach their ends.
Inputs may be any that keep to these rules, and one draw needn't show every extreme that they name: `expert_ids`: in each device's block of 128 rows no expert is named more than 80 times.
All inputs are finite; a program needn't handle non-finite values.
Results may differ from the reference program's by a relative error of at most 0.014.
Values may be sent and summed in bfloat16 or wider, within the bound.
A program may use at most 128 MiB of HBM per device.

```python
import math
import jax
import jax.numpy as jnp
import numpy as np
from jax import lax

D = 3584
HID = 1024
TOP = 8
TOK_DEV = 128
EXPERTS = 16
CAP = 80
SLOTS = 2560
TOKENS = 4096
N_EXPERT = 16
N_REPLICA = 2


def draw_hidden(key, part):
    first, second = jax.random.split(key, 2)
    ramp = 0.6 + 1.2 * jnp.arange(HID, dtype=jnp.float32) / HID
    columns = ramp * jnp.exp(jax.random.uniform(second, (HID,), jnp.float32, -0.4, 0.4))
    values = jnp.clip(jax.random.normal(first, (EXPERTS, SLOTS, HID), jnp.float32), -4.0, 4.0)
    return (values * columns).astype(jnp.bfloat16)


def shard_levels(key, shape, cuts, least, largest):
    factor_of = 1.0
    for dim, parts in cuts:
        draws = jax.random.uniform(jax.random.fold_in(jax.random.fold_in(key, 6), dim), (parts,), jnp.float32, least / len(cuts), largest / len(cuts))
        factor_of = factor_of * jnp.repeat(jnp.exp(draws), shape[dim] // parts).reshape((-1,) + (1,) * (len(shape) - 1 - dim))
    return factor_of


def deal_out(key, own, number, rows, amount, top, limit, lean):
    sequence = jax.random.permutation(key, amount)
    packed, usual = load_shares(amount, rows * top, limit, lean, True), load_shares(amount, rows * top, limit, lean, False)
    places = jnp.arange(amount)

    def named(tallies, offset_by):
        used = int((tallies > 0).sum())
        fixed = max(1, used // 4)
        shifted = fixed + (places - fixed + offset_by * (used - fixed)) % max(1, amount - fixed)
        return jnp.zeros((amount,), jnp.int32).at[sequence[jnp.where(places < fixed, places, shifted)]].set(jnp.asarray(tallies, jnp.int32))

    tallies = jnp.where(number % 4 == 0, named(packed, number // 4), named(usual, number - number // 4 - 1))
    mixed = jax.random.permutation(jax.random.fold_in(own, 3), amount)
    donor, receiver = mixed[0:amount // 2 * 2:2], mixed[1:amount // 2 * 2:2]
    slack = jnp.minimum(tallies[donor] - 1, limit - tallies[receiver]) // 2
    slack = jnp.where((donor == sequence[0]) | (receiver == sequence[0]) | (tallies[receiver] == 0), 0, jnp.maximum(slack, 0))
    shifted = jax.random.randint(jax.random.fold_in(own, 4), (amount // 2,), 0, 1 << 20) % (slack + 1)
    tallies = tallies.at[donor].add(-shifted).at[receiver].add(shifted)
    labels = jnp.searchsorted(jnp.cumsum(tallies), jnp.arange(rows * top), side="right").astype(jnp.int32)
    table = labels.reshape(top, rows).T
    table = table[jax.random.permutation(jax.random.fold_in(own, 1), rows)]
    offset_by = jax.random.randint(jax.random.fold_in(own, 2), (rows, 1), 0, top)
    return jnp.take_along_axis(table, (jnp.arange(top)[None, :] + offset_by) % top, axis=1)


def load_shares(number_of, total, bound, skew, full):
    portions = [(1 << 20) // math.isqrt(rank ** skew) + 1 for rank in range(1, number_of + 1)]
    largest = bound if full else min(bound, max(-(-total // number_of), total * portions[0] // sum(portions)))
    least = 1 if total - largest >= number_of - 1 else 0
    holding, rest = [largest] + [least] * (number_of - 1), total - largest - least * (number_of - 1)
    while rest > 0:
        movable = [i for i in range(1, number_of) if holding[i] < largest] or [i for i in range(1, number_of) if holding[i] < bound]
        mass, budget = sum([portions[i] for i in movable]), rest
        for i in movable:
            extra = min(bound - holding[i], max(1, budget * portions[i] // mass), rest)
            holding[i] = holding[i] + extra
            rest = rest - extra
    return np.array(holding)


def scatter_about(own_key, shape, deviation, bound, cuts=(), kind=jnp.bfloat16):
    values = jax.random.normal(own_key, shape, jnp.float32) * deviation
    if len(cuts) > 0:
        values = shard_levels(own_key, shape, cuts, -0.22, 0.18) * values
    return jnp.clip(values, min=-bound, max=bound).astype(kind)


def setup_inputs(seed: int = 0) -> dict:
    splits = jax.random.split(jax.random.key(seed), 7)
    grad_tokens = scatter_about(splits[0], (TOKENS, D), 0.25, 1.5, ((0, 32),))
    gates = jnp.clip(jnp.exp(math.log(0.3) - 2.7080503 * jax.random.uniform(splits[1], (TOKENS, TOP), jnp.float32) ** shard_levels(splits[1], (TOKENS, TOP), ((0, 32),), -0.2, 0.2)), 0.02, 0.3)
    expert_ids_keys = jax.random.split(jax.random.fold_in(splits[2], 1), TOKENS // TOK_DEV)
    expert_ids_turns = jax.random.permutation(jax.random.fold_in(splits[2], 3), TOKENS // TOK_DEV)
    expert_ids = jax.vmap(lambda own, number: deal_out(jax.random.fold_in(splits[2], 2), own, number, TOK_DEV, EXPERTS, TOP, CAP, 2))(expert_ids_keys, expert_ids_turns).reshape((TOKENS, TOP))
    hidden = draw_hidden(jax.random.fold_in(splits[6], 71), 0)
    row_moment = jnp.clip(jnp.exp(math.log(1.0) - 2.3025851 * jax.random.uniform(splits[4], (EXPERTS, HID), jnp.float32) ** shard_levels(splits[4], (EXPERTS, HID), ((0, 16), (1, 2)), -0.2, 0.2)), 0.1, 1.0)
    col_moment = jnp.clip(jnp.exp(math.log(1.0) - 2.3025851 * jax.random.uniform(splits[5], (EXPERTS, D), jnp.float32) ** shard_levels(splits[5], (EXPERTS, D), ((0, 16),), -0.2, 0.2)), 0.1, 1.0)
    return {"grad_tokens": grad_tokens, "gates": gates, "expert_ids": expert_ids, "hidden": hidden, "row_moment": row_moment, "col_moment": col_moment}


DECAY_RATE = 0.9
EPSILON = 1e-06

def adafactor(gradient, row_old, col_old):
    squares = gradient * gradient
    row_out = DECAY_RATE * row_old + (1.0 - DECAY_RATE) * (lax.optimization_barrier(jnp.mean(squares, axis=1)) + EPSILON)
    col_out = DECAY_RATE * col_old + (1.0 - DECAY_RATE) * (lax.optimization_barrier(jnp.mean(squares, axis=0)) + EPSILON)
    scaled = gradient / jnp.sqrt(row_out[:, None] * col_out[None, :])
    spread = jnp.sqrt(jnp.mean(scaled * scaled))
    return ((scaled / jnp.maximum(1.0, spread)).astype(jnp.bfloat16), row_out, col_out)

def reference(grad_tokens, gates, expert_ids, hidden, row_moment, col_moment):
    assigned = TOK_DEV * TOP
    block_ids = expert_ids.reshape(N_EXPERT, N_REPLICA, assigned)
    onehot = (block_ids[..., None] == jnp.arange(EXPERTS, dtype=jnp.int32)).astype(jnp.int32)
    position = lax.optimization_barrier(jnp.sum((jnp.cumsum(onehot, axis=2) - onehot) * onehot, axis=3))
    position = position.reshape(N_EXPERT, N_REPLICA, TOK_DEV, TOP).astype(jnp.int32)
    chosen_ids = expert_ids.reshape(N_EXPERT, N_REPLICA, TOK_DEV, TOP)
    weights_all = gates.reshape(N_EXPERT, N_REPLICA, TOK_DEV, TOP)
    token_grads = jnp.moveaxis(grad_tokens.reshape(N_EXPERT, N_REPLICA, TOK_DEV, D), 1, 0)
    stored = hidden.reshape(EXPERTS, N_REPLICA, N_EXPERT * CAP, HID)
    source_base = (jnp.arange(N_EXPERT, dtype=jnp.int32) * CAP)[:, None, None]

    def one_expert(expert):
        chosen = chosen_ids == expert
        scale_of = lax.optimization_barrier(jnp.sum(jnp.where(chosen, weights_all, jnp.float32(0.0)), axis=3))
        slot = lax.optimization_barrier(jnp.sum(jnp.where(chosen, position, 0), axis=3)).astype(jnp.int32)
        target = jnp.where(jnp.any(chosen, axis=3), source_base + slot, N_EXPERT * CAP).astype(jnp.int32)
        expert_hidden = lax.dynamic_index_in_dim(stored, expert, 0, keepdims=False)

        def one_replica(total, inputs):
            grads_here, scale_here, target_here, hidden_here = inputs
            sent_rows = (scale_here[..., None] * grads_here.astype(jnp.float32)).astype(jnp.bfloat16)
            sent_rows = sent_rows.reshape(N_EXPERT * TOK_DEV, D)
            buffer = jnp.zeros((N_EXPERT * CAP, D), jnp.bfloat16)
            buffer = buffer.at[target_here.reshape(-1)].add(sent_rows, mode='drop')
            partial_value = jnp.dot(hidden_here.T, buffer, preferred_element_type=jnp.float32).astype(jnp.bfloat16)
            return (total + partial_value.astype(jnp.float32), None)
        inputs = (token_grads, jnp.moveaxis(scale_of, 1, 0), jnp.moveaxis(target, 1, 0), expert_hidden)
        gradient, unused = lax.scan(one_replica, jnp.zeros((HID, D), jnp.float32), inputs)
        return adafactor(gradient, row_moment[expert], col_moment[expert])
    update, row_new, col_new = lax.map(one_expert, jnp.arange(EXPERTS, dtype=jnp.int32))
    return (update, row_new, col_new)
```

```python
import functools

import jax
import jax.numpy as jnp
from jax import lax
from jax.experimental import pallas as pl
from jax.experimental.pallas import tpu as pltpu
from jax.sharding import PartitionSpec as P

DECAY_RATE = 0.9
EPSILON = 1e-06
MESH = pl.DeviceIdType.MESH
LANES = 128
PAIR = 2 * LANES


def grid_of(count):
    line = 4 if count % 4 == 0 else 1
    rest, bits = count // line, []
    while rest > 1:
        if rest % 2:
            return count, []
        rest //= 2
        bits.append(rest)
    return line, bits


def chunk_plan(tiles, bits, rounds):
    forward = list(range(len(bits)))
    backward = forward[::-1]
    orders = [["line"] + backward, ["line"] + forward, backward + ["line"], forward + ["line"]]
    pairs = tiles // 2
    plan, start = [], 0
    for index in range(rounds):
        stop = 2 * (pairs * (index + 1) // rounds)
        count = stop - start
        late = max(2, round(count * 3 / 14))
        left = count - late
        sizes = [0, 0, 0, 0]
        sizes[index % 2] = left - left // 2
        sizes[1 - index % 2] = left // 2
        sizes[2 + index % 2] = late - late // 2
        sizes[3 - index % 2] = late // 2
        at = start
        pieces = []
        for order, size in zip(orders, sizes):
            if size > 0:
                pieces.append((at, size, order))
                at += size
        plan.append(pieces)
        start = stop
    return plan


def kernel(cfg, meta_hbm, tok_hbm, hid_hbm, row_ref, col_ref, upd_hbm, row_out, col_out,
           tok, meta, hid, hid_t, onehot, weight, sent, part, got, grad, row_acc, cols, cols_got,
           sem_in, sem_meta_s, sem_meta_r, sem_s, sem_r, sem_part_s, sem_part_r, sem_col_s,
           sem_col_r, sem_out):
    experts, replicas, line, bits, plan, starts, cap, share = cfg
    expert = lax.axis_index("expert")
    replica = lax.axis_index("replica")
    stride = experts // line
    place = expert // stride
    inner = expert % stride
    tiles = tok.shape[0]
    pairs = tiles // 2
    width = tiles * LANES
    hidden_total = share * replicas

    table = [sorted((q for q in range(line) if q != p), key=lambda q: (abs(q - p), q)) for p in range(line)]

    def line_source(rank):
        if rank == 0:
            return place
        value = jnp.int32(0)
        for p in range(line):
            value = value + jnp.where(place == p, jnp.int32(table[p][rank - 1]), 0)
        return value

    line_of = [line_source(rank) for rank in range(line)]

    def flipped(index, bit):
        digit = (index // bits[bit]) % 2
        return index + bits[bit] * (1 - 2 * digit)

    def source_of(rank, mask):
        where = inner
        for bit in range(len(bits)):
            if mask >> bit & 1:
                where = flipped(where, bit)
        return line_of[rank] * stride + where

    copies = []

    def load(src, dst, sem):
        copy = pltpu.make_async_copy(src, dst, sem)
        copy.start()
        return copy

    loads = []
    for tile in range(tiles):
        loads.append(load(tok_hbm.at[:, pl.ds(tile * LANES, LANES)], tok.at[tile, expert], sem_in.at[tile]))
    load_meta = load(meta_hbm, meta.at[expert], sem_in.at[tiles])
    load_hid = load(hid_hbm, hid, sem_in.at[tiles + 1])

    barrier = pltpu.get_barrier_semaphore()
    right_ok, left_ok = place + 1 < line, place > 0
    if line > 1:
        @pl.when(right_ok)
        def _():
            pl.semaphore_signal(barrier, inc=1, device_id=(expert + stride, replica), device_id_type=MESH)

        @pl.when(left_ok)
        def _():
            pl.semaphore_signal(barrier, inc=1, device_id=(expert - stride, replica), device_id_type=MESH)
    for bit in range(len(bits)):
        peer = place * stride + flipped(inner, bit)
        pl.semaphore_signal(barrier, inc=1, device_id=(peer, replica), device_id_type=MESH)
    for k in range(1, replicas):
        pl.semaphore_signal(barrier, inc=1, device_id=(expert, lax.rem(replica + k, replicas)), device_id_type=MESH)
    expected = len(bits) + replicas - 1 + jnp.where(right_ok, 1, 0) + jnp.where(left_ok, 1, 0)
    pl.semaphore_wait(barrier, expected)

    counters = {"tok": 0, "meta": 0}

    def send(piece, first, source, target, valid):
        start, size, _ = plan_flat[piece]
        pieces = [(tok.at[pl.ds(start, size), source], sem_s.at[counters["tok"]], sem_r.at[piece, source])]
        counters["tok"] += 1
        if first:
            pieces.append((meta.at[source], sem_meta_s.at[counters["meta"]], sem_meta_r.at[source]))
            counters["meta"] += 1

        def go():
            for ref, s_sem, r_sem in pieces:
                pltpu.make_async_remote_copy(ref, ref, s_sem, r_sem, device_id=(target, replica), device_id_type=MESH).start()

        def done():
            for ref, s_sem, r_sem in pieces:
                pltpu.make_async_remote_copy(ref, ref, s_sem, r_sem, device_id=(target, replica), device_id_type=MESH).wait_send()

        if valid is None:
            go()
        else:
            pl.when(valid)(go)
        copies.append((done, valid))

    plan_flat = [piece for pieces in plan for piece in pieces]

    def forward(piece, rank, mask):
        order = plan_flat[piece][2]
        source = source_of(rank, mask)
        at = -1
        for step, dim in enumerate(order):
            if (dim == "line" and rank > 0) or (dim != "line" and mask >> dim & 1):
                at = step
        for step, dim in enumerate(order):
            if dim == "line" and line > 1 and step >= at:
                if rank == 0:
                    send(piece, piece == 0, source, expert + stride, right_ok)
                    send(piece, piece == 0, source, expert - stride, left_ok)
                elif rank < line - 0:
                    up = line_of[rank] < place
                    target = jnp.where(up, expert + stride, expert - stride)
                    valid = jnp.where(up, place + 1 < line, place > 0)
                    send(piece, piece == 0, source, target, valid)
            elif dim != "line" and step > at:
                peer = place * stride + flipped(inner, dim)
                send(piece, piece == 0, source, peer, None)

    def arrive(piece, rank, mask):
        start, size, _ = plan_flat[piece]
        source = source_of(rank, mask)
        ref = tok.at[pl.ds(start, size), source]
        pltpu.make_async_remote_copy(ref, ref, sem_s.at[0], sem_r.at[piece, source], device_id=(expert, replica), device_id_type=MESH).wait_recv()
        if piece == 0:
            ref = meta.at[source]
            pltpu.make_async_remote_copy(ref, ref, sem_meta_s.at[0], sem_meta_r.at[source], device_id=(expert, replica), device_id_type=MESH).wait_recv()

    def transpose_hidden():
        block = PAIR
        for row in range(hid.shape[0] // block):
            for col in range(hid.shape[1] // block):
                hid_t[col * block:(col + 1) * block, row * block:(row + 1) * block] = jnp.transpose(
                    hid[row * block:(row + 1) * block, col * block:(col + 1) * block]
                )

    def route():
        values = meta[...]
        choices = values.shape[1] // 2
        tokens = values.shape[2]
        match = values[:, :choices, :] == expert.astype(jnp.float32)
        named = jnp.sum(jnp.where(match, 1.0, 0.0), axis=1)
        scale = jnp.sum(jnp.where(match, values[:, choices:, :], 0.0), axis=1)
        earlier = lax.broadcasted_iota(jnp.int32, (tokens, tokens), 0) < lax.broadcasted_iota(jnp.int32, (tokens, tokens), 1)
        position = jnp.dot(named.astype(jnp.bfloat16), jnp.where(earlier, 1.0, 0.0).astype(jnp.bfloat16), preferred_element_type=jnp.float32)
        slot = jnp.where(named > 0.5, position, -1.0 - 2.0 * cap)
        rows = lax.broadcasted_iota(jnp.int32, (2 * cap, tokens), 0).astype(jnp.float32)
        for pair in range(experts // 2):
            total = 0.0
            for half in range(2):
                source = 2 * pair + half
                hit = rows == slot[source:source + 1, :] + float(half * cap)
                onehot[pair, :, half * tokens:(half + 1) * tokens] = jnp.where(hit, 1.0, 0.0).astype(jnp.bfloat16)
                total = total + jnp.sum(jnp.where(hit, scale[source:source + 1, :], 0.0), axis=1, keepdims=True)
            weight[pair] = jnp.broadcast_to(total, (2 * cap, LANES))

    def compute(q):
        for pair in range(experts // 2):
            tokens = tok.shape[2]
            block = [tok[2 * q + half, 2 * pair:2 * pair + 2].reshape(2 * tokens, LANES) for half in range(2)]
            rows = jnp.dot(onehot[pair], jnp.concatenate(block, axis=1), preferred_element_type=jnp.float32)
            scale = weight[pair]
            sent[pair * 2 * cap:(pair + 1) * 2 * cap, :] = (rows * jnp.concatenate([scale, scale], axis=1)).astype(jnp.bfloat16)
        values = sent[...]
        step = min(share, 256)
        for owner in range(replicas):
            for at in range(0, share, step):
                low = owner * share + at
                part[q, owner, at:at + step, :] = jnp.dot(hid_t[low:low + step, :], values, preferred_element_type=jnp.float32).astype(jnp.bfloat16)

    def part_copy(q, k):
        peer = lax.rem(replica + k, replicas)
        return pltpu.make_async_remote_copy(part.at[q, peer], got.at[q, replica], sem_part_s.at[q, k], sem_part_r.at[q, replica], device_id=(expert, peer), device_id_type=MESH)

    def part_send(q):
        for k in range(1, replicas):
            part_copy(q, k).start()

    def columns(q):
        return pl.ds(pl.multiple_of(q * PAIR, PAIR), PAIR)

    def collect(q):
        total = part[q, replica].astype(jnp.float32)
        for k in range(1, replicas):
            peer = lax.rem(replica + k, replicas)
            pltpu.make_async_remote_copy(got.at[q, peer], got.at[q, peer], sem_part_s.at[q, k], sem_part_r.at[q, peer], device_id=(expert, peer), device_id_type=MESH).wait_recv()
            total = total + got[q, peer].astype(jnp.float32)
        grad[q] = total
        squares = total * total
        row_acc[...] = row_acc[...] + squares[:, :LANES] + squares[:, LANES:]
        cols[0:1, columns(q)] = jnp.sum(squares, axis=0, keepdims=True)

    def step(q):
        compute(q)
        pl.when(q >= 1)(lambda: part_send(q - 1))
        pl.when(q >= 3)(lambda: collect(q - 3))

    def steps(low, high):
        if high > low:
            def run(q, carry):
                step(q)
                return carry
            lax.fori_loop(low, high, run, 0)

    for copy in loads:
        copy.wait()
    load_meta.wait()
    gap = 4
    events = []
    base = 0
    for index, pieces in enumerate(plan):
        for order_at in range(len(pieces)):
            piece = base + order_at
            for rank in range(line):
                for mask in range(1 << len(bits)):
                    wave = rank + bin(mask).count("1") + gap * index
                    events.append((wave, index, rank, mask, piece))
        base += len(pieces)
    events.sort()
    remaining = [sum(1 for e in events if e[1] == index) for index in range(len(plan))]
    ends = [pieces[-1][0] + pieces[-1][1] for pieces in plan]
    ready, done_steps = 0, 0
    prepared = False
    hidden_ready = False
    events_left = len(events)
    since = 0
    for wave, index, rank, mask, piece in events:
        if rank or mask:
            arrive(piece, rank, mask)
        forward(piece, rank, mask)
        events_left -= 1
        since += 1
        remaining[index] -= 1
        if not hidden_ready and wave >= 1:
            load_hid.wait()
            transpose_hidden()
            row_acc[...] = jnp.zeros_like(row_acc)
            hidden_ready = True
        if remaining[index] == 0:
            ready = ends[index] // 2
            if not prepared:
                route()
                prepared = True
            since = 0
        elif done_steps < ready and since >= 6:
            run_to = min(ready, done_steps + 1)
            steps(done_steps, run_to)
            done_steps = run_to
            since = 0
    steps(done_steps, pairs)
    part_send(pairs - 1)
    for q in range(max(0, pairs - 3), pairs):
        collect(q)

    old_row = jnp.transpose(jnp.broadcast_to(row_ref[...], (LANES, share)))[:, :1]
    row_new = DECAY_RATE * old_row + (1.0 - DECAY_RATE) * (jnp.sum(row_acc[...], axis=1, keepdims=True) / width + EPSILON)
    row_inverse = 1.0 / row_new

    def ratio(q, carry):
        values = grad[q]
        cols[1:2, columns(q)] = jnp.sum(values * values * row_inverse, axis=0, keepdims=True)
        return carry

    lax.fori_loop(0, pairs, ratio, 0)
    row_out[...] = jnp.transpose(jnp.broadcast_to(row_new, (share, LANES)))[0:1, :]
    row_scale = 1.0 / jnp.sqrt(row_new)

    def col_copy(k):
        peer = lax.rem(replica + k, replicas)
        return pltpu.make_async_remote_copy(cols, cols_got.at[replica], sem_col_s.at[k], sem_col_r.at[replica], device_id=(expert, peer), device_id_type=MESH)

    for k in range(1, replicas):
        col_copy(k).start()
    total = cols[...]
    for done, valid in copies:
        if valid is None:
            done()
        else:
            pl.when(valid)(done)

    def drain(q, carry):
        for k in range(1, replicas):
            part_copy(q, k).wait_send()
        return carry

    lax.fori_loop(0, pairs, drain, 0)
    for k in range(1, replicas):
        peer = lax.rem(replica + k, replicas)
        pltpu.make_async_remote_copy(cols, cols_got.at[peer], sem_col_s.at[k], sem_col_r.at[peer], device_id=(expert, peer), device_id_type=MESH).wait_recv()
        total = total + cols_got[peer]
    for k in range(1, replicas):
        col_copy(k).wait_send()
    col_new = DECAY_RATE * col_ref[...] + (1.0 - DECAY_RATE) * (total[0:1] / hidden_total + EPSILON)
    col_out[...] = col_new
    spread = jnp.sqrt(jnp.sum(total[1:2] / col_new, axis=1, keepdims=True) / (hidden_total * width))
    cols[0:1, :] = 1.0 / (jnp.sqrt(col_new) * jnp.maximum(1.0, spread))

    def out_copy(q):
        return pltpu.make_async_copy(part.at[q, 0], upd_hbm.at[:, columns(q)], sem_out.at[q])

    def finish(q, carry):
        part[q, 0] = (grad[q] * row_scale * cols[0:1, columns(q)]).astype(jnp.bfloat16)
        out_copy(q).start()
        return carry

    def settle(q, carry):
        out_copy(q).wait()
        return carry

    lax.fori_loop(0, pairs, finish, 0)
    lax.fori_loop(0, pairs, settle, 0)


def body(grad_tokens, gates, expert_ids, hidden, row_moment, col_moment):
    experts = lax.axis_size("expert")
    replicas = lax.axis_size("replica")
    choices = expert_ids.shape[1]
    tokens, width = grad_tokens.shape
    slots, hidden_total = hidden.shape[1:]
    cap = slots // experts
    share = hidden_total // replicas
    line, bits = grid_of(experts)
    tiles = width // LANES
    plan = chunk_plan(tiles, bits, 2)
    pieces = sum(len(p) for p in plan)
    pairs = tiles // 2
    sends = pieces * experts * (len(bits) + 2)
    meta = jnp.concatenate([expert_ids.T.astype(jnp.float32), gates.T], axis=0)
    dma = pltpu.SemaphoreType.DMA
    vmem = pl.BlockSpec(memory_space=pltpu.VMEM)
    anywhere = pl.BlockSpec(memory_space=pl.ANY)
    cfg = (experts, replicas, line, bits, plan, None, cap, share)
    update, row_new, col_new = pl.pallas_call(
        functools.partial(kernel, cfg),
        name="routed_down_backward",
        out_shape=(
            jax.ShapeDtypeStruct((share, width), jnp.bfloat16),
            jax.ShapeDtypeStruct((1, share), jnp.float32),
            jax.ShapeDtypeStruct((1, width), jnp.float32),
        ),
        in_specs=[anywhere, anywhere, anywhere, vmem, vmem],
        out_specs=(anywhere, vmem, vmem),
        scratch_shapes=[
            pltpu.VMEM((tiles, experts, tokens, LANES), jnp.bfloat16),
            pltpu.VMEM((experts, 2 * choices, tokens), jnp.float32),
            pltpu.VMEM((slots, hidden_total), jnp.bfloat16),
            pltpu.VMEM((hidden_total, slots), jnp.bfloat16),
            pltpu.VMEM((experts // 2, 2 * cap, 2 * tokens), jnp.bfloat16),
            pltpu.VMEM((experts // 2, 2 * cap, LANES), jnp.float32),
            pltpu.VMEM((slots, PAIR), jnp.bfloat16),
            pltpu.VMEM((pairs, replicas, share, PAIR), jnp.bfloat16),
            pltpu.VMEM((pairs, replicas, share, PAIR), jnp.bfloat16),
            pltpu.VMEM((pairs, share, PAIR), jnp.float32),
            pltpu.VMEM((share, LANES), jnp.float32),
            pltpu.VMEM((2, width), jnp.float32),
            pltpu.VMEM((replicas, 2, width), jnp.float32),
            dma((tiles + 2,)),
            dma((experts * (len(bits) + 2),)),
            dma((experts,)),
            dma((sends,)),
            dma((pieces, experts)),
            dma((pairs, replicas)),
            dma((pairs, replicas)),
            dma((replicas,)),
            dma((replicas,)),
            dma((pairs,)),
        ],
        compiler_params=pltpu.CompilerParams(
            collective_id=0, has_side_effects=True, vmem_limit_bytes=62 * 1024 * 1024
        ),
    )(meta, grad_tokens, hidden[0], row_moment, col_moment)
    return (update[None], row_new, col_new)


def solution(mesh):
    placed = (
        P(("expert", "replica"), None),
        P(("expert", "replica"), None),
        P(("expert", "replica"), None),
        P("expert", "replica", None),
        P("expert", "replica"),
        P("expert", None),
    )
    return jax.shard_map(
        body,
        mesh=mesh,
        in_specs=placed,
        out_specs=(P("expert", "replica", None), P("expert", "replica"), P("expert", None)),
        check_vma=False,
    )
```

```python
import functools

import jax
import jax.numpy as jnp
from jax import lax
from jax.experimental import pallas as pl
from jax.experimental.pallas import tpu as pltpu
from jax.sharding import PartitionSpec as P

DECAY_RATE = 0.9
EPSILON = 1e-06
MESH = pl.DeviceIdType.MESH
LANES = 128
PAIR = 2 * LANES
ROUNDS = 2
LATE = 2 / 7
GAP = 3
EVERY = 2


def grid_of(count):
    line = 4 if count % 4 == 0 else 1
    rest, bits = count // line, []
    while rest > 1:
        if rest % 2:
            return count, []
        rest //= 2
        bits.append(rest)
    return line, bits


def chunk_plan(tiles, bits, rounds):
    forward = list(range(len(bits)))
    backward = forward[::-1]
    orders = [["line"] + backward, ["line"] + forward]
    orders += [way[:-1] + ["line"] + way[-1:] for way in (backward, forward)]
    pairs = tiles // 2
    plan, start = [], 0
    for index in range(rounds):
        stop = 2 * (pairs * (index + 1) // rounds)
        count = stop - start
        late = max(2, round(count * LATE))
        left = count - late
        sizes = [0, 0, 0, 0]
        sizes[index % 2] = left - left // 2
        sizes[1 - index % 2] = left // 2
        sizes[2 + index % 2] = late - late // 2
        sizes[3 - index % 2] = late // 2
        at = start
        pieces = []
        for order, size in zip(orders, sizes):
            if size > 0:
                pieces.append((at, size, order))
                at += size
        plan.append(pieces)
        start = stop
    return plan


def kernel(cfg, meta_hbm, tok_hbm, hid_hbm, row_ref, col_ref, upd_hbm, row_out, col_out,
           tok, meta, hid, hid_t, onehot, weight, earlier, sent, stage, part, got, grad, row_acc, cols, cols_got,
           sem_in, sem_meta_s, sem_meta_r, sem_s, sem_r, sem_part_s, sem_part_r, sem_col_s,
           sem_col_r, sem_out):
    experts, replicas, line, bits, plan, starts, cap, share = cfg
    expert = lax.axis_index("expert")
    replica = lax.axis_index("replica")
    stride = experts // line
    place = expert // stride
    inner = expert % stride
    tiles = tok.shape[0]
    pairs = tiles // 2
    width = tiles * LANES
    hidden_total = share * replicas

    table = [sorted((q for q in range(line) if q != p), key=lambda q: (abs(q - p), q)) for p in range(line)]

    def line_source(rank):
        if rank == 0:
            return place
        value = jnp.int32(0)
        for p in range(line):
            value = value + jnp.where(place == p, jnp.int32(table[p][rank - 1]), 0)
        return value

    line_of = [line_source(rank) for rank in range(line)]

    def flipped(index, bit):
        digit = (index // bits[bit]) % 2
        return index + bits[bit] * (1 - 2 * digit)

    def source_of(rank, mask):
        where = inner
        for bit in range(len(bits)):
            if mask >> bit & 1:
                where = flipped(where, bit)
        return line_of[rank] * stride + where

    copies = []

    def load(src, dst, sem):
        copy = pltpu.make_async_copy(src, dst, sem)
        copy.start()
        return copy

    lasts = [bits[0], bits[-1]]

    def side(piece):
        return lasts.index(bits[plan_flat[piece][2][-1]])

    def block_of(source, way):
        low = lasts[way]
        return (source // (2 * low)) * low + source % low

    plan_flat = [piece for pieces in plan for piece in pieces]
    loads = []
    for piece, (start, size, _) in enumerate(plan_flat):
        for tile in range(start, start + size):
            loads.append(load(tok_hbm.at[:, pl.ds(tile * LANES, LANES)], tok.at[tile, block_of(expert, side(piece))], sem_in.at[tile]))
    load_meta = [load(meta_hbm, meta.at[way, block_of(expert, way)], sem_in.at[tiles + 2 + way]) for way in range(2)]
    load_hid = load(hid_hbm, hid, sem_in.at[tiles + 1])

    barrier = pltpu.get_barrier_semaphore()
    right_ok, left_ok = place + 1 < line, place > 0
    if line > 1:
        @pl.when(right_ok)
        def _():
            pl.semaphore_signal(barrier, inc=1, device_id=(expert + stride, replica), device_id_type=MESH)

        @pl.when(left_ok)
        def _():
            pl.semaphore_signal(barrier, inc=1, device_id=(expert - stride, replica), device_id_type=MESH)
    for bit in range(len(bits)):
        peer = place * stride + flipped(inner, bit)
        pl.semaphore_signal(barrier, inc=1, device_id=(peer, replica), device_id_type=MESH)
    for k in range(1, replicas):
        pl.semaphore_signal(barrier, inc=1, device_id=(expert, lax.rem(replica + k, replicas)), device_id_type=MESH)
    expected = len(bits) + replicas - 1 + jnp.where(right_ok, 1, 0) + jnp.where(left_ok, 1, 0)
    pl.semaphore_wait(barrier, expected)

    counters = {"tok": 0, "meta": 0}
    pending = []

    def send(parts, target, valid):
        def each(act):
            for src, dst, s_sem, r_sem in parts:
                act(pltpu.make_async_remote_copy(src, dst, s_sem, r_sem, device_id=(target, replica), device_id_type=MESH))

        def go():
            each(lambda copy: copy.start())

        def done():
            each(lambda copy: copy.wait_send())

        copies.append((done, valid))
        return go if valid is None else (lambda: pl.when(valid)(go))

    def next_sem():
        counters["tok"] += 1
        return sem_s.at[counters["tok"] - 1]

    def raw_parts(piece, source):
        start, size, _ = plan_flat[piece]
        way = side(piece)
        ref = tok.at[pl.ds(start, size), block_of(source, way)]
        parts = [(ref, ref, next_sem(), sem_r.at[piece, source])]
        if piece < 2:
            ref = meta.at[way, block_of(source, way)]
            parts.append((ref, ref, sem_meta_s.at[way, counters["meta"]], sem_meta_r.at[way, source]))
            counters["meta"] += 1
        return parts

    def forward(piece, rank, mask):
        order = plan_flat[piece][2][:-1]
        source = source_of(rank, mask)
        at = -1
        for step, dim in enumerate(order):
            if (dim == "line" and rank > 0) or (dim != "line" and mask >> dim & 1):
                at = step
        for step, dim in enumerate(order):
            if dim == "line" and line > 1 and step >= at:
                if rank == 0:
                    send(raw_parts(piece, source), expert + stride, right_ok)()
                    send(raw_parts(piece, source), expert - stride, left_ok)()
                elif rank < line:
                    up = line_of[rank] < place
                    target = jnp.where(up, expert + stride, expert - stride)
                    send(raw_parts(piece, source), target, jnp.where(up, place + 1 < line, place > 0))()
            elif dim != "line" and step > at:
                send(raw_parts(piece, source), place * stride + flipped(inner, dim), None)()

    def landed(ref, sem):
        pltpu.make_async_remote_copy(ref, ref, sem_s.at[0], sem, device_id=(expert, replica), device_id_type=MESH).wait_recv()

    def leaf(piece, mask):
        return mask >> plan_flat[piece][2][-1] & 1

    def arrive(piece, rank, mask):
        start, size, _ = plan_flat[piece]
        source = source_of(rank, mask)
        way = side(piece)
        if leaf(piece, mask):
            landed(sent.at[pl.ds(start, size), source], sem_r.at[piece, source])
            return
        landed(tok.at[pl.ds(start, size), block_of(source, way)], sem_r.at[piece, source])
        if piece < 2:
            landed(meta.at[way, block_of(source, way)], sem_meta_r.at[way, source])

    def peer_of(way):
        return place * stride + flipped(inner, bits.index(lasts[way]))

    def route(way, source):
        block = block_of(source, way)
        values = meta[way, block]
        choices = values.shape[0] // 2
        tokens = values.shape[1]
        named, scale = [], []
        for target in (expert, peer_of(way)):
            match = values[:choices, :] == target.astype(jnp.float32)
            named.append(jnp.sum(jnp.where(match, 1.0, 0.0), axis=0, keepdims=True))
            scale.append(jnp.sum(jnp.where(match, values[choices:, :], 0.0), axis=0, keepdims=True))
        both = jnp.concatenate([jnp.broadcast_to(row, (8, tokens)) for row in named], axis=0)
        position = jnp.dot(both.astype(jnp.bfloat16), earlier[...], preferred_element_type=jnp.float32)
        rows = lax.broadcasted_iota(jnp.int32, (cap, tokens), 0).astype(jnp.float32)
        for half in range(2):
            slot = jnp.where(named[half] > 0.5, position[8 * half:8 * half + 1], -1.0)
            hit = rows == slot
            onehot[way, block, half * cap:(half + 1) * cap, :] = jnp.where(hit, 1.0, 0.0).astype(jnp.bfloat16)
            total = jnp.sum(jnp.where(hit, scale[half], 0.0), axis=1, keepdims=True)
            weight[way, block, half * cap:(half + 1) * cap, :] = jnp.broadcast_to(total, (cap, LANES))

    def pack(piece, rank, mask):
        start, size, _ = plan_flat[piece]
        way = side(piece)
        source = source_of(rank, mask)
        block = block_of(source, way)
        if piece < 2:
            route(way, source)
        hits = onehot[way, block]
        scale = weight[way, block]
        for low in range(start, start + size, 2):
            count = min(2, start + size - low)
            columns_in = [tok[low + k, block] for k in range(count)]
            rows = jnp.dot(hits, jnp.concatenate(columns_in, axis=1), preferred_element_type=jnp.float32)
            for k in range(count):
                out = (rows[:, k * LANES:(k + 1) * LANES] * scale).astype(jnp.bfloat16)
                sent[low + k, source] = out[:cap]
                stage[low + k, block] = out[cap:]
        parts = [(stage.at[pl.ds(start, size), block], sent.at[pl.ds(start, size), source], next_sem(), sem_r.at[piece, source])]
        flush()
        pending.append(send(parts, peer_of(way), None))

    def flush():
        while pending:
            pending.pop()()

    def transpose_hidden():
        block = PAIR
        for row in range(hid.shape[0] // block):
            for col in range(hid.shape[1] // block):
                hid_t[col * block:(col + 1) * block, row * block:(row + 1) * block] = jnp.transpose(
                    hid[row * block:(row + 1) * block, col * block:(col + 1) * block]
                )

    def compute(q):
        values = jnp.concatenate([sent[2 * q + k].reshape(experts * cap, LANES) for k in range(2)], axis=1)
        step = min(share, 256)
        for owner in range(replicas):
            for at in range(0, share, step):
                low = owner * share + at
                part[q, owner, at:at + step, :] = jnp.dot(hid_t[low:low + step, :], values, preferred_element_type=jnp.float32).astype(jnp.bfloat16)

    def part_copy(q, k):
        peer = lax.rem(replica + k, replicas)
        return pltpu.make_async_remote_copy(part.at[q, peer], got.at[q, replica], sem_part_s.at[q, k], sem_part_r.at[q, replica], device_id=(expert, peer), device_id_type=MESH)

    def part_send(q):
        for k in range(1, replicas):
            part_copy(q, k).start()

    def columns(q):
        return pl.ds(pl.multiple_of(q * PAIR, PAIR), PAIR)

    def collect(q):
        total = part[q, replica].astype(jnp.float32)
        for k in range(1, replicas):
            peer = lax.rem(replica + k, replicas)
            pltpu.make_async_remote_copy(got.at[q, peer], got.at[q, peer], sem_part_s.at[q, k], sem_part_r.at[q, peer], device_id=(expert, peer), device_id_type=MESH).wait_recv()
            total = total + got[q, peer].astype(jnp.float32)
        grad[q] = total
        squares = total * total
        row_acc[...] = row_acc[...] + squares[:, :LANES] + squares[:, LANES:]
        cols[0:1, columns(q)] = jnp.sum(squares, axis=0, keepdims=True)

    def step(q):
        compute(q)
        pl.when(q >= 1)(lambda: part_send(q - 1))
        pl.when(q >= 3)(lambda: collect(q - 3))

    def steps(low, high):
        if high > low:
            def run(q, carry):
                step(q)
                return carry
            lax.fori_loop(low, high, run, 0)

    tokens = meta.shape[3]
    before = lax.broadcasted_iota(jnp.int32, (tokens, tokens), 0) < lax.broadcasted_iota(jnp.int32, (tokens, tokens), 1)
    earlier[...] = jnp.where(before, 1.0, 0.0).astype(jnp.bfloat16)
    for copy in load_meta + loads:
        copy.wait()
    gap = GAP
    events = []
    base = 0
    for index, pieces in enumerate(plan):
        for order_at in range(len(pieces)):
            piece = base + order_at
            for rank in range(line):
                for mask in range(1 << len(bits)):
                    wave = rank + bin(mask).count("1") + gap * index
                    if leaf(piece, mask):
                        wave = line + len(bits) + gap * index
                    events.append((wave, index, rank, mask, piece))
        base += len(pieces)
    events.sort()
    remaining = [sum(1 for e in events if e[1] == index) for index in range(len(plan))]
    ends = [pieces[-1][0] + pieces[-1][1] for pieces in plan]
    ready, done_steps, since, hidden_ready = 0, 0, 0, False
    raw_left = sum(1 for e in events if not leaf(e[4], e[3]))
    for wave, index, rank, mask, piece in events:
        if rank or mask:
            arrive(piece, rank, mask)
        remaining[index] -= 1
        if not leaf(piece, mask):
            forward(piece, rank, mask)
            pack(piece, rank, mask)
            since += 1
            raw_left -= 1
            if raw_left == 0:
                flush()
        if not hidden_ready and wave >= 1:
            load_hid.wait()
            transpose_hidden()
            row_acc[...] = jnp.zeros_like(row_acc)
            hidden_ready = True
        if remaining[index] == 0:
            ready = ends[index] // 2
            since = EVERY
        if done_steps < ready and since >= EVERY and index + 1 < len(plan) + (remaining[-1] > 0):
            steps(done_steps, done_steps + 1)
            done_steps += 1
            since = 0
    steps(done_steps, pairs)
    part_send(pairs - 1)
    for q in range(max(0, pairs - 3), pairs):
        collect(q)

    old_row = jnp.transpose(jnp.broadcast_to(row_ref[...], (LANES, share)))[:, :1]
    row_new = DECAY_RATE * old_row + (1.0 - DECAY_RATE) * (jnp.sum(row_acc[...], axis=1, keepdims=True) / width + EPSILON)
    row_inverse = 1.0 / row_new

    def ratio(q, carry):
        values = grad[q]
        cols[1:2, columns(q)] = jnp.sum(values * values * row_inverse, axis=0, keepdims=True)
        return carry

    lax.fori_loop(0, pairs, ratio, 0)
    row_out[...] = jnp.transpose(jnp.broadcast_to(row_new, (share, LANES)))[0:1, :]
    row_scale = 1.0 / jnp.sqrt(row_new)

    def col_copy(k):
        peer = lax.rem(replica + k, replicas)
        return pltpu.make_async_remote_copy(cols, cols_got.at[replica], sem_col_s.at[k], sem_col_r.at[replica], device_id=(expert, peer), device_id_type=MESH)

    for k in range(1, replicas):
        col_copy(k).start()
    total = cols[...]
    for done, valid in copies:
        if valid is None:
            done()
        else:
            pl.when(valid)(done)

    def drain(q, carry):
        for k in range(1, replicas):
            part_copy(q, k).wait_send()
        return carry

    lax.fori_loop(0, pairs, drain, 0)
    for k in range(1, replicas):
        peer = lax.rem(replica + k, replicas)
        pltpu.make_async_remote_copy(cols, cols_got.at[peer], sem_col_s.at[k], sem_col_r.at[peer], device_id=(expert, peer), device_id_type=MESH).wait_recv()
        total = total + cols_got[peer]
    for k in range(1, replicas):
        col_copy(k).wait_send()
    col_new = DECAY_RATE * col_ref[...] + (1.0 - DECAY_RATE) * (total[0:1] / hidden_total + EPSILON)
    col_out[...] = col_new
    spread = jnp.sqrt(jnp.sum(total[1:2] / col_new, axis=1, keepdims=True) / (hidden_total * width))
    cols[0:1, :] = 1.0 / (jnp.sqrt(col_new) * jnp.maximum(1.0, spread))

    def out_copy(q):
        return pltpu.make_async_copy(part.at[q, 0], upd_hbm.at[:, columns(q)], sem_out.at[q])

    def finish(q, carry):
        part[q, 0] = (grad[q] * row_scale * cols[0:1, columns(q)]).astype(jnp.bfloat16)
        out_copy(q).start()
        return carry

    def settle(q, carry):
        out_copy(q).wait()
        return carry

    lax.fori_loop(0, pairs, finish, 0)
    lax.fori_loop(0, pairs, settle, 0)


def body(grad_tokens, gates, expert_ids, hidden, row_moment, col_moment):
    experts = lax.axis_size("expert")
    replicas = lax.axis_size("replica")
    choices = expert_ids.shape[1]
    tokens, width = grad_tokens.shape
    slots, hidden_total = hidden.shape[1:]
    cap = slots // experts
    local_hidden = hidden[0]
    if cap % 16:
        padded = cap + 16 - cap % 16
        local_hidden = jnp.pad(
            local_hidden.reshape(experts, cap, hidden_total), ((0, 0), (0, padded - cap), (0, 0))
        ).reshape(experts * padded, hidden_total)
        cap, slots = padded, experts * padded
    share = hidden_total // replicas
    line, bits = grid_of(experts)
    tiles = width // LANES
    plan = chunk_plan(tiles, bits, ROUNDS)
    pieces = sum(len(p) for p in plan)
    pairs = tiles // 2
    sends = pieces * experts * (len(bits) + 2)
    meta = jnp.concatenate([expert_ids.T.astype(jnp.float32), gates.T], axis=0)
    dma = pltpu.SemaphoreType.DMA
    vmem = pl.BlockSpec(memory_space=pltpu.VMEM)
    anywhere = pl.BlockSpec(memory_space=pl.ANY)
    cfg = (experts, replicas, line, bits, plan, None, cap, share)
    update, row_new, col_new = pl.pallas_call(
        functools.partial(kernel, cfg),
        name="routed_down_backward",
        out_shape=(
            jax.ShapeDtypeStruct((share, width), jnp.bfloat16),
            jax.ShapeDtypeStruct((1, share), jnp.float32),
            jax.ShapeDtypeStruct((1, width), jnp.float32),
        ),
        in_specs=[anywhere, anywhere, anywhere, vmem, vmem],
        out_specs=(anywhere, vmem, vmem),
        scratch_shapes=[
            pltpu.VMEM((tiles, experts // 2, tokens, LANES), jnp.bfloat16),
            pltpu.VMEM((2, experts // 2, 2 * choices, tokens), jnp.float32),
            pltpu.VMEM((slots, hidden_total), jnp.bfloat16),
            pltpu.VMEM((hidden_total, slots), jnp.bfloat16),
            pltpu.VMEM((2, experts // 2, 2 * cap, tokens), jnp.bfloat16),
            pltpu.VMEM((2, experts // 2, 2 * cap, LANES), jnp.float32),
            pltpu.VMEM((tokens, tokens), jnp.bfloat16),
            pltpu.VMEM((tiles, experts, cap, LANES), jnp.bfloat16),
            pltpu.VMEM((tiles, experts // 2, cap, LANES), jnp.bfloat16),
            pltpu.VMEM((pairs, replicas, share, PAIR), jnp.bfloat16),
            pltpu.VMEM((pairs, replicas, share, PAIR), jnp.bfloat16),
            pltpu.VMEM((pairs, share, PAIR), jnp.float32),
            pltpu.VMEM((share, LANES), jnp.float32),
            pltpu.VMEM((2, width), jnp.float32),
            pltpu.VMEM((replicas, 2, width), jnp.float32),
            dma((tiles + 4,)),
            dma((2, 2 * experts * (len(bits) + 2))),
            dma((2, experts)),
            dma((sends,)),
            dma((pieces, experts)),
            dma((pairs, replicas)),
            dma((pairs, replicas)),
            dma((replicas,)),
            dma((replicas,)),
            dma((pairs,)),
        ],
        compiler_params=pltpu.CompilerParams(
            collective_id=0, has_side_effects=True, vmem_limit_bytes=62 * 1024 * 1024
        ),
    )(meta, grad_tokens, local_hidden, row_moment, col_moment)
    return (update[None], row_new, col_new)


def solution(mesh):
    placed = (
        P(("expert", "replica"), None),
        P(("expert", "replica"), None),
        P(("expert", "replica"), None),
        P("expert", "replica", None),
        P("expert", "replica"),
        P("expert", None),
    )
    return jax.shard_map(
        body,
        mesh=mesh,
        in_specs=placed,
        out_specs=(P("expert", "replica", None), P("expert", "replica"), P("expert", None)),
        check_vma=False,
    )
```

```python
import functools

import jax
import jax.numpy as jnp
from jax import lax
from jax.experimental import pallas as pl
from jax.experimental.pallas import tpu as pltpu
from jax.sharding import PartitionSpec as P

DECAY_RATE = 0.9
EPSILON = 1e-06
MESH = pl.DeviceIdType.MESH
LANES = 128
PAIR = 2 * LANES
ROUNDS = 2
LATE = 2 / 7
GAP = 3
EVERY = 2


def grid_of(count):
    line = 4 if count % 4 == 0 else 1
    rest, bits = count // line, []
    while rest > 1:
        if rest % 2:
            return count, []
        rest //= 2
        bits.append(rest)
    return line, bits


def chunk_plan(tiles, bits, rounds):
    forward = list(range(len(bits)))
    backward = forward[::-1]
    orders = [["line"] + backward, ["line"] + forward]
    orders += [way[:-1] + ["line"] + way[-1:] for way in (backward, forward)]
    pairs = tiles // 2
    plan, start = [], 0
    for index in range(rounds):
        stop = tiles if index + 1 == rounds else 2 * (pairs * (index + 1) * 9 // (rounds * 7))
        count = stop - start
        late = max(2, round(count * LATE))
        left = count - late
        sizes = [0, 0, 0, 0]
        sizes[index % 2] = left - left // 2
        sizes[1 - index % 2] = left // 2
        sizes[2 + index % 2] = late - late // 2
        sizes[3 - index % 2] = late // 2
        at = start
        pieces = []
        for order, size in zip(orders, sizes):
            if size > 0:
                pieces.append((at, size, order))
                at += size
        plan.append(pieces)
        start = stop
    return plan


def kernel(cfg, meta_hbm, tok_hbm, hid_hbm, row_ref, col_ref, upd_hbm, row_out, col_out,
           tok, meta, hid, hid_t, onehot, weight, earlier, sent, stage, part, got, grad, row_acc, cols, cols_got,
           sem_in, sem_meta_s, sem_meta_r, sem_s, sem_r, sem_part_s, sem_part_r, sem_col_s,
           sem_col_r, sem_out):
    experts, replicas, line, bits, plan, starts, cap, share = cfg
    expert = lax.axis_index("expert")
    replica = lax.axis_index("replica")
    stride = experts // line
    place = expert // stride
    inner = expert % stride
    tiles = tok.shape[0]
    pairs = tiles // 2
    width = tiles * LANES
    hidden_total = share * replicas

    table = [sorted((q for q in range(line) if q != p), key=lambda q: (abs(q - p), q)) for p in range(line)]

    def line_source(rank):
        if rank == 0:
            return place
        value = jnp.int32(0)
        for p in range(line):
            value = value + jnp.where(place == p, jnp.int32(table[p][rank - 1]), 0)
        return value

    line_of = [line_source(rank) for rank in range(line)]

    def flipped(index, bit):
        digit = (index // bits[bit]) % 2
        return index + bits[bit] * (1 - 2 * digit)

    def source_of(rank, mask):
        where = inner
        for bit in range(len(bits)):
            if mask >> bit & 1:
                where = flipped(where, bit)
        return line_of[rank] * stride + where

    copies = []

    def load(src, dst, sem):
        copy = pltpu.make_async_copy(src, dst, sem)
        copy.start()
        return copy

    lasts = [bits[0], bits[-1]]

    def side(piece):
        return lasts.index(bits[plan_flat[piece][2][-1]])

    def block_of(source, way):
        low = lasts[way]
        return (source // (2 * low)) * low + source % low

    plan_flat = [piece for pieces in plan for piece in pieces]
    loads = []
    for piece, (start, size, _) in enumerate(plan_flat):
        for tile in range(start, start + size):
            loads.append(load(tok_hbm.at[:, pl.ds(tile * LANES, LANES)], tok.at[tile, block_of(expert, side(piece))], sem_in.at[tile]))
    load_meta = [load(meta_hbm, meta.at[way, block_of(expert, way)], sem_in.at[tiles + 2 + way]) for way in range(2)]
    load_hid = load(hid_hbm, hid, sem_in.at[tiles + 1])

    barrier = pltpu.get_barrier_semaphore()
    right_ok, left_ok = place + 1 < line, place > 0
    if line > 1:
        @pl.when(right_ok)
        def _():
            pl.semaphore_signal(barrier, inc=1, device_id=(expert + stride, replica), device_id_type=MESH)

        @pl.when(left_ok)
        def _():
            pl.semaphore_signal(barrier, inc=1, device_id=(expert - stride, replica), device_id_type=MESH)
    for bit in range(len(bits)):
        peer = place * stride + flipped(inner, bit)
        pl.semaphore_signal(barrier, inc=1, device_id=(peer, replica), device_id_type=MESH)
    for k in range(1, replicas):
        pl.semaphore_signal(barrier, inc=1, device_id=(expert, lax.rem(replica + k, replicas)), device_id_type=MESH)
    expected = len(bits) + replicas - 1 + jnp.where(right_ok, 1, 0) + jnp.where(left_ok, 1, 0)
    pl.semaphore_wait(barrier, expected)

    counters = {"tok": 0, "meta": 0}
    pending = []

    def send(parts, target, valid):
        def each(act):
            for src, dst, s_sem, r_sem in parts:
                act(pltpu.make_async_remote_copy(src, dst, s_sem, r_sem, device_id=(target, replica), device_id_type=MESH))

        def go():
            each(lambda copy: copy.start())

        def done():
            each(lambda copy: copy.wait_send())

        copies.append((done, valid))
        return go if valid is None else (lambda: pl.when(valid)(go))

    def next_sem():
        counters["tok"] += 1
        return sem_s.at[counters["tok"] - 1]

    def raw_parts(piece, source):
        start, size, _ = plan_flat[piece]
        way = side(piece)
        ref = tok.at[pl.ds(start, size), block_of(source, way)]
        parts = [(ref, ref, next_sem(), sem_r.at[piece, source])]
        if piece < 2:
            ref = meta.at[way, block_of(source, way)]
            parts.append((ref, ref, sem_meta_s.at[way, counters["meta"]], sem_meta_r.at[way, source]))
            counters["meta"] += 1
        return parts

    def forward(piece, rank, mask):
        order = plan_flat[piece][2][:-1]
        source = source_of(rank, mask)
        at = -1
        for step, dim in enumerate(order):
            if (dim == "line" and rank > 0) or (dim != "line" and mask >> dim & 1):
                at = step
        for step, dim in enumerate(order):
            if dim == "line" and line > 1 and step >= at:
                if rank == 0:
                    send(raw_parts(piece, source), expert + stride, right_ok)()
                    send(raw_parts(piece, source), expert - stride, left_ok)()
                elif rank < line:
                    up = line_of[rank] < place
                    target = jnp.where(up, expert + stride, expert - stride)
                    send(raw_parts(piece, source), target, jnp.where(up, place + 1 < line, place > 0))()
            elif dim != "line" and step > at:
                send(raw_parts(piece, source), place * stride + flipped(inner, dim), None)()

    def landed(ref, sem):
        pltpu.make_async_remote_copy(ref, ref, sem_s.at[0], sem, device_id=(expert, replica), device_id_type=MESH).wait_recv()

    def leaf(piece, mask):
        return mask >> plan_flat[piece][2][-1] & 1

    def arrive(piece, rank, mask):
        start, size, _ = plan_flat[piece]
        source = source_of(rank, mask)
        way = side(piece)
        if leaf(piece, mask):
            landed(sent.at[pl.ds(start, size), source], sem_r.at[piece, source])
            return
        landed(tok.at[pl.ds(start, size), block_of(source, way)], sem_r.at[piece, source])
        if piece < 2:
            landed(meta.at[way, block_of(source, way)], sem_meta_r.at[way, source])

    def peer_of(way):
        return place * stride + flipped(inner, bits.index(lasts[way]))

    def route(way, source):
        block = block_of(source, way)
        values = meta[way, block]
        choices = values.shape[0] // 2
        tokens = values.shape[1]
        named, scale = [], []
        for target in (expert, peer_of(way)):
            match = values[:choices, :] == target.astype(jnp.float32)
            named.append(jnp.sum(jnp.where(match, 1.0, 0.0), axis=0, keepdims=True))
            scale.append(jnp.sum(jnp.where(match, values[choices:, :], 0.0), axis=0, keepdims=True))
        both = jnp.concatenate([jnp.broadcast_to(row, (8, tokens)) for row in named], axis=0)
        position = jnp.dot(both.astype(jnp.bfloat16), earlier[...], preferred_element_type=jnp.float32)
        rows = lax.broadcasted_iota(jnp.int32, (cap, tokens), 0).astype(jnp.float32)
        for half in range(2):
            slot = jnp.where(named[half] > 0.5, position[8 * half:8 * half + 1], -1.0)
            hit = rows == slot
            onehot[way, block, half * cap:(half + 1) * cap, :] = jnp.where(hit, 1.0, 0.0).astype(jnp.bfloat16)
            total = jnp.sum(jnp.where(hit, scale[half], 0.0), axis=1, keepdims=True)
            weight[way, block, half * cap:(half + 1) * cap, :] = jnp.broadcast_to(total, (cap, LANES))

    def pack(piece, rank, mask):
        start, size, _ = plan_flat[piece]
        way = side(piece)
        source = source_of(rank, mask)
        block = block_of(source, way)
        if piece < 2:
            route(way, source)
        hits = onehot[way, block]
        scale = weight[way, block]
        for low in range(start, start + size, 2):
            count = min(2, start + size - low)
            columns_in = [tok[low + k, block] for k in range(count)]
            rows = jnp.dot(hits, jnp.concatenate(columns_in, axis=1), preferred_element_type=jnp.float32)
            for k in range(count):
                out = (rows[:, k * LANES:(k + 1) * LANES] * scale).astype(jnp.bfloat16)
                sent[low + k, source] = out[:cap]
                stage[low + k, block] = out[cap:]
        parts = [(stage.at[pl.ds(start, size), block], sent.at[pl.ds(start, size), source], next_sem(), sem_r.at[piece, source])]
        flush()
        pending.append(send(parts, peer_of(way), None))

    def flush():
        while pending:
            pending.pop()()

    def transpose_hidden():
        block = PAIR
        for row in range(hid.shape[0] // block):
            for col in range(hid.shape[1] // block):
                hid_t[col * block:(col + 1) * block, row * block:(row + 1) * block] = jnp.transpose(
                    hid[row * block:(row + 1) * block, col * block:(col + 1) * block]
                )

    def compute(q):
        values = jnp.concatenate([sent[2 * q + k].reshape(experts * cap, LANES) for k in range(2)], axis=1)
        step = min(share, 256)
        for owner in range(replicas):
            for at in range(0, share, step):
                low = owner * share + at
                part[q, owner, at:at + step, :] = jnp.dot(hid_t[low:low + step, :], values, preferred_element_type=jnp.float32).astype(jnp.bfloat16)

    def part_copy(q, k):
        peer = lax.rem(replica + k, replicas)
        return pltpu.make_async_remote_copy(part.at[q, peer], got.at[q, replica], sem_part_s.at[q, k], sem_part_r.at[q, replica], device_id=(expert, peer), device_id_type=MESH)

    def part_send(q):
        for k in range(1, replicas):
            part_copy(q, k).start()

    def columns(q):
        return pl.ds(pl.multiple_of(q * PAIR, PAIR), PAIR)

    def collect(q):
        total = part[q, replica].astype(jnp.float32)
        for k in range(1, replicas):
            peer = lax.rem(replica + k, replicas)
            pltpu.make_async_remote_copy(got.at[q, peer], got.at[q, peer], sem_part_s.at[q, k], sem_part_r.at[q, peer], device_id=(expert, peer), device_id_type=MESH).wait_recv()
            total = total + got[q, peer].astype(jnp.float32)
        grad[q] = total
        squares = total * total
        row_acc[...] = row_acc[...] + squares[:, :LANES] + squares[:, LANES:]
        cols[0:1, columns(q)] = jnp.sum(squares, axis=0, keepdims=True)

    def step(q):
        compute(q)
        pl.when(q >= 1)(lambda: part_send(q - 1))
        pl.when(q >= 3)(lambda: collect(q - 3))

    def steps(low, high):
        if high > low:
            def run(q, carry):
                step(q)
                return carry
            lax.fori_loop(low, high, run, 0)

    tokens = meta.shape[3]
    before = lax.broadcasted_iota(jnp.int32, (tokens, tokens), 0) < lax.broadcasted_iota(jnp.int32, (tokens, tokens), 1)
    earlier[...] = jnp.where(before, 1.0, 0.0).astype(jnp.bfloat16)
    for copy in load_meta + loads:
        copy.wait()
    gap = GAP
    events = []
    base = 0
    for index, pieces in enumerate(plan):
        for order_at in range(len(pieces)):
            piece = base + order_at
            for rank in range(line):
                for mask in range(1 << len(bits)):
                    wave = rank + bin(mask).count("1") + gap * index
                    if leaf(piece, mask):
                        wave = line + len(bits) + gap * index
                    events.append((wave, index, rank, mask, piece))
        base += len(pieces)
    events.sort()
    remaining = [sum(1 for e in events if e[1] == index) for index in range(len(plan))]
    ends = [pieces[-1][0] + pieces[-1][1] for pieces in plan]
    ready, done_steps, since, hidden_ready = 0, 0, 0, False
    raw_left = sum(1 for e in events if not leaf(e[4], e[3]))
    for wave, index, rank, mask, piece in events:
        if rank or mask:
            arrive(piece, rank, mask)
        remaining[index] -= 1
        if not leaf(piece, mask):
            forward(piece, rank, mask)
            pack(piece, rank, mask)
            since += 1
            raw_left -= 1
            if raw_left == 0:
                flush()
        if not hidden_ready and wave >= 1:
            load_hid.wait()
            transpose_hidden()
            row_acc[...] = jnp.zeros_like(row_acc)
            hidden_ready = True
        if remaining[index] == 0:
            ready = ends[index] // 2
            since = EVERY
        if done_steps < ready and since >= EVERY and index + 1 < len(plan) + (remaining[-1] > 0):
            steps(done_steps, done_steps + 1)
            done_steps += 1
            since = 0
    steps(done_steps, pairs)
    part_send(pairs - 1)
    for q in range(max(0, pairs - 3), pairs):
        collect(q)

    old_row = jnp.transpose(jnp.broadcast_to(row_ref[...], (LANES, share)))[:, :1]
    row_new = DECAY_RATE * old_row + (1.0 - DECAY_RATE) * (jnp.sum(row_acc[...], axis=1, keepdims=True) / width + EPSILON)
    row_inverse = 1.0 / row_new

    def ratio(q, carry):
        values = grad[q]
        cols[1:2, columns(q)] = jnp.sum(values * values * row_inverse, axis=0, keepdims=True)
        return carry

    lax.fori_loop(0, pairs, ratio, 0)
    row_out[...] = jnp.transpose(jnp.broadcast_to(row_new, (share, LANES)))[0:1, :]
    row_scale = 1.0 / jnp.sqrt(row_new)

    def col_copy(k):
        peer = lax.rem(replica + k, replicas)
        return pltpu.make_async_remote_copy(cols, cols_got.at[replica], sem_col_s.at[k], sem_col_r.at[replica], device_id=(expert, peer), device_id_type=MESH)

    for k in range(1, replicas):
        col_copy(k).start()
    total = cols[...]
    for done, valid in copies:
        if valid is None:
            done()
        else:
            pl.when(valid)(done)

    def drain(q, carry):
        for k in range(1, replicas):
            part_copy(q, k).wait_send()
        return carry

    lax.fori_loop(0, pairs, drain, 0)
    for k in range(1, replicas):
        peer = lax.rem(replica + k, replicas)
        pltpu.make_async_remote_copy(cols, cols_got.at[peer], sem_col_s.at[k], sem_col_r.at[peer], device_id=(expert, peer), device_id_type=MESH).wait_recv()
        total = total + cols_got[peer]
    for k in range(1, replicas):
        col_copy(k).wait_send()
    col_new = DECAY_RATE * col_ref[...] + (1.0 - DECAY_RATE) * (total[0:1] / hidden_total + EPSILON)
    col_out[...] = col_new
    spread = jnp.sqrt(jnp.sum(total[1:2] / col_new, axis=1, keepdims=True) / (hidden_total * width))
    cols[0:1, :] = 1.0 / (jnp.sqrt(col_new) * jnp.maximum(1.0, spread))

    def out_copy(q):
        return pltpu.make_async_copy(part.at[q, 0], upd_hbm.at[:, columns(q)], sem_out.at[q])

    def finish(q, carry):
        part[q, 0] = (grad[q] * row_scale * cols[0:1, columns(q)]).astype(jnp.bfloat16)
        out_copy(q).start()
        return carry

    def settle(q, carry):
        out_copy(q).wait()
        return carry

    lax.fori_loop(0, pairs, finish, 0)
    lax.fori_loop(0, pairs, settle, 0)


def body(grad_tokens, gates, expert_ids, hidden, row_moment, col_moment):
    experts = lax.axis_size("expert")
    replicas = lax.axis_size("replica")
    choices = expert_ids.shape[1]
    tokens, width = grad_tokens.shape
    slots, hidden_total = hidden.shape[1:]
    cap = slots // experts
    local_hidden = hidden[0]
    if cap % 16:
        padded = cap + 16 - cap % 16
        local_hidden = jnp.pad(
            local_hidden.reshape(experts, cap, hidden_total), ((0, 0), (0, padded - cap), (0, 0))
        ).reshape(experts * padded, hidden_total)
        cap, slots = padded, experts * padded
    share = hidden_total // replicas
    line, bits = grid_of(experts)
    tiles = width // LANES
    plan = chunk_plan(tiles, bits, ROUNDS)
    pieces = sum(len(p) for p in plan)
    pairs = tiles // 2
    sends = pieces * experts * (len(bits) + 2)
    meta = jnp.concatenate([expert_ids.T.astype(jnp.float32), gates.T], axis=0)
    dma = pltpu.SemaphoreType.DMA
    vmem = pl.BlockSpec(memory_space=pltpu.VMEM)
    anywhere = pl.BlockSpec(memory_space=pl.ANY)
    cfg = (experts, replicas, line, bits, plan, None, cap, share)
    update, row_new, col_new = pl.pallas_call(
        functools.partial(kernel, cfg),
        name="routed_down_backward",
        out_shape=(
            jax.ShapeDtypeStruct((share, width), jnp.bfloat16),
            jax.ShapeDtypeStruct((1, share), jnp.float32),
            jax.ShapeDtypeStruct((1, width), jnp.float32),
        ),
        in_specs=[anywhere, anywhere, anywhere, vmem, vmem],
        out_specs=(anywhere, vmem, vmem),
        scratch_shapes=[
            pltpu.VMEM((tiles, experts // 2, tokens, LANES), jnp.bfloat16),
            pltpu.VMEM((2, experts // 2, 2 * choices, tokens), jnp.float32),
            pltpu.VMEM((slots, hidden_total), jnp.bfloat16),
            pltpu.VMEM((hidden_total, slots), jnp.bfloat16),
            pltpu.VMEM((2, experts // 2, 2 * cap, tokens), jnp.bfloat16),
            pltpu.VMEM((2, experts // 2, 2 * cap, LANES), jnp.float32),
            pltpu.VMEM((tokens, tokens), jnp.bfloat16),
            pltpu.VMEM((tiles, experts, cap, LANES), jnp.bfloat16),
            pltpu.VMEM((tiles, experts // 2, cap, LANES), jnp.bfloat16),
            pltpu.VMEM((pairs, replicas, share, PAIR), jnp.bfloat16),
            pltpu.VMEM((pairs, replicas, share, PAIR), jnp.bfloat16),
            pltpu.VMEM((pairs, share, PAIR), jnp.float32),
            pltpu.VMEM((share, LANES), jnp.float32),
            pltpu.VMEM((2, width), jnp.float32),
            pltpu.VMEM((replicas, 2, width), jnp.float32),
            dma((tiles + 4,)),
            dma((2, 2 * experts * (len(bits) + 2))),
            dma((2, experts)),
            dma((sends,)),
            dma((pieces, experts)),
            dma((pairs, replicas)),
            dma((pairs, replicas)),
            dma((replicas,)),
            dma((replicas,)),
            dma((pairs,)),
        ],
        compiler_params=pltpu.CompilerParams(
            collective_id=0, has_side_effects=True, vmem_limit_bytes=62 * 1024 * 1024
        ),
    )(meta, grad_tokens, local_hidden, row_moment, col_moment)
    return (update[None], row_new, col_new)


def solution(mesh):
    placed = (
        P(("expert", "replica"), None),
        P(("expert", "replica"), None),
        P(("expert", "replica"), None),
        P("expert", "replica", None),
        P("expert", "replica"),
        P("expert", None),
    )
    return jax.shard_map(
        body,
        mesh=mesh,
        in_specs=placed,
        out_specs=(P("expert", "replica", None), P("expert", "replica"), P("expert", None)),
        check_vma=False,
    )
```
